128 devices in a mesh: ta: 8 (over z_hi, y), ha: 2 (over core), wa: 8 (over z_lo, x).
Axes of the slice: x: 4, y: 4, z: 4 (z_hi: 2, z_lo: 2; z = z_hi * 2 + z_lo), core: 2. Of those that a mesh axis runs over, the one named last changes fastest.
Arguments:
- queries: bfloat16 [32, 32, 64, 768], P('ta', 'ha', 'wa'), may hold values from -64 to 64
- keys: bfloat16 [32, 32, 64, 768], P('ta', 'ha', 'wa'), may hold values from -4 to 4
- values: bfloat16 [32, 32, 64, 768], P('ta', 'ha', 'wa'), may hold values from -6 to 6
- text_keys: bfloat16 [256, 768], P(('ta', 'ha', 'wa')), may hold values from -5 to 5
- text_values: bfloat16 [256, 768], P(('ta', 'ha', 'wa')), may hold values from -6 to 6
Outputs:
- attended: bfloat16 [32, 32, 64, 768], P('ta', 'ha', 'wa')
The draws below stay inside these ranges and needn't reach their ends.
All inputs are finite; a program needn't handle non-finite values.
Results may differ from the reference program's by a relative error of at most 0.0037.
Values may be sent and summed in bfloat16 or wider, within the bound.
No kernel may reach another device: no remote copies, remote signals or barrier semaphores. Data moves between devices by JAX's collectives and lax.ppermute only.
A program may use at most 192 MiB of HBM per device.

```python
import jax
import jax.numpy as jnp
from jax import lax

HEADS = 6
HD = 128
TEXT = 256
TILE_T = 4
TILE_H = 8
TILE_W = 8
C = 768
NT = 32
NH = 32
NW = 64


def shared_fields(key):
    shape = (NT, NH, NW, HEADS * HD)
    key_field = jnp.clip(jax.random.normal(jax.random.fold_in(key, 11), shape, jnp.float32), -4.0, 4.0)
    query_field = jnp.clip(2.0 * jax.random.normal(jax.random.fold_in(key, 12), shape, jnp.float32), -8.0, 8.0)
    return (query_field, key_field)


def draw_queries(key, part):
    return shared_fields(key)[0].astype(jnp.bfloat16)


def draw_keys(key, part):
    return shared_fields(key)[1].astype(jnp.bfloat16)


def level_of(key, shape, pieces, smallest, largest):
    gain, own = 1.0, jax.random.fold_in(key, 6)
    for position, parts in pieces:
        draws = jnp.exp(jax.random.uniform(jax.random.fold_in(own, position), (parts,), jnp.float32, smallest / len(pieces), largest / len(pieces)))
        gain = gain * jnp.repeat(draws, shape[position] // parts).reshape([-1 if axis == position else 1 for axis in range(len(shape))])
    return gain


def gaussian(own_key, dims, width, bound, shards=(), held_as=jnp.bfloat16):
    array = jax.random.normal(own_key, dims, jnp.float32) * width
    if len(shards) > 0:
        array = level_of(own_key, dims, shards, -0.22, 0.18) * array
    return jnp.clip(array, min=-bound, max=bound).astype(held_as)


def setup_inputs(seed: int = 0) -> dict:
    key_list = jax.random.split(jax.random.key(seed), 6)
    return {
        "queries": draw_queries(jax.random.fold_in(key_list[5], 71), 0),
        "keys": draw_keys(jax.random.fold_in(key_list[5], 71), 0),
        "values": gaussian(key_list[2], (NT, NH, NW, C), 1.0, 6.0, ((0, 8), (1, 2), (2, 8))),
        "text_keys": gaussian(key_list[3], (TEXT, C), 1.0, 5.0, ((0, 128),)),
        "text_values": gaussian(key_list[4], (TEXT, C), 1.0, 6.0, ((0, 128),)),
    }


def attend(query_tile, key_tile, value_tile, keep, text_keys, text_values):
    keys_all = jnp.concatenate([key_tile, text_keys], 0).astype(jnp.float32)
    vals_all = jnp.concatenate([value_tile, text_values], 0).astype(jnp.float32)
    scores = jnp.einsum("qhd,khd->hqk", query_tile.astype(jnp.float32), keys_all) * (query_tile.shape[2] ** -0.5)
    allowed = jnp.concatenate([keep, jnp.ones((text_keys.shape[0],), jnp.float32) > 0.5])
    scores = jnp.where(allowed[None, None, :], scores, jnp.float32(-1e30))
    top = jnp.max(scores, -1, keepdims=True)
    weights = jnp.exp(scores - top)
    total = jnp.sum(weights, -1)
    rounded = weights.astype(jnp.bfloat16).astype(jnp.float32)
    summed = jnp.einsum("hqk,khd->qhd", rounded, vals_all)
    return (summed / jnp.transpose(total)[:, :, None]).astype(jnp.bfloat16)


def inside_tiles(count):
    place = jnp.arange(count + 2, dtype=jnp.int32) - 1
    return ((place >= 0) & (place < count)).astype(jnp.float32)


def reference(queries, keys, values, text_keys, text_values):
    count_t = NT // TILE_T
    count_h = NH // TILE_H
    count_w = NW // TILE_W
    shape7 = (count_t, TILE_T, count_h, TILE_H, count_w, TILE_W, HEADS * HD)
    grid_q = queries.reshape(shape7)
    pads = ((1, 1), (0, 0), (1, 1), (0, 0), (1, 1), (0, 0), (0, 0))
    grid_k = jnp.pad(keys.reshape(shape7), pads)
    grid_v = jnp.pad(values.reshape(shape7), pads)
    keep_t = inside_tiles(count_t)
    keep_h = inside_tiles(count_h)
    keep_w = inside_tiles(count_w)
    text_k = text_keys.reshape(TEXT, HEADS, HD)
    text_v = text_values.reshape(TEXT, HEADS, HD)
    zero = jnp.int32(0)

    def one_tile(flat):
        tile_a = flat // (count_h * count_w)
        tile_b = (flat // count_w) % count_h
        tile_c = flat % count_w
        start = (tile_a, zero, tile_b, zero, tile_c, zero, zero)
        query_tile = lax.dynamic_slice(grid_q, start, (1, TILE_T, 1, TILE_H, 1, TILE_W, HEADS * HD)).reshape(-1, HEADS, HD)
        size = (3, TILE_T, 3, TILE_H, 3, TILE_W, HEADS * HD)
        key_tile = lax.dynamic_slice(grid_k, start, size).reshape(-1, HEADS, HD)
        value_tile = lax.dynamic_slice(grid_v, start, size).reshape(-1, HEADS, HD)
        part_t = lax.dynamic_slice_in_dim(keep_t, tile_a, 3)
        part_h = lax.dynamic_slice_in_dim(keep_h, tile_b, 3)
        part_w = lax.dynamic_slice_in_dim(keep_w, tile_c, 3)
        mask = part_t[:, None, None, None, None, None] * part_h[None, None, :, None, None, None] * part_w[None, None, None, None, :, None]
        mask = jnp.broadcast_to(mask, (3, TILE_T, 3, TILE_H, 3, TILE_W)).reshape(-1) > 0.5
        return attend(query_tile, key_tile, value_tile, mask, text_k, text_v)

    tiles = lax.map(one_tile, jnp.arange(count_t * count_h * count_w, dtype=jnp.int32))
    tiles = tiles.reshape(count_t, count_h, count_w, TILE_T, TILE_H, TILE_W, HEADS * HD)
    tiles = jnp.transpose(tiles, (0, 3, 1, 4, 2, 5, 6))
    return tiles.reshape(NT, NH, NW, HEADS * HD)
```

```python
import functools

import jax
import jax.numpy as jnp
from jax import lax
from jax.experimental import pallas as pl
from jax.experimental.pallas import tpu as pltpu
from jax.sharding import PartitionSpec as P

HEADS = 6
TILE_T = 4
TILE_H = 8
TILE_W = 8
HD = 128
ROWS = 256
STAT_ROWS = 32
LOG2E = 1.4426950408889634
NEG = -1e30
CHUNKS = ((0, 3), (3, 5), (5, 6))
TEXT_PAD = 2


def dot_nt(a, b):
    return lax.dot_general(a, b, (((1,), (1,)), ((), ())), preferred_element_type=jnp.float32)


def split3(x):
    hi = x.astype(jnp.bfloat16).astype(jnp.float32)
    mid = (x - hi).astype(jnp.bfloat16).astype(jnp.float32)
    low = x - hi - mid
    return hi, mid, low


def attend_kernel(scale, flags, qo, ql, qr, k, v, km, kp, bo, bt, text, oo, os, ol, orr, qs, kx, vx, kbx, vbx, tx):
    bnd = flags[0]
    oks = [None, flags[1] > 0, flags[2] > 0]
    for w, ref in enumerate((qo, ql, qr)):
        for role in range(2):
            hb = bnd if role == 0 else 1 - bnd
            qs[w, role] = ref[:, hb].reshape(ROWS, HD)
    ones = jnp.ones((2 * ROWS, HD), jnp.bfloat16)
    for j, (kr, vr) in enumerate(((k, v), (km.at[0], km.at[1]), (kp.at[0], kp.at[1]))):
        kx[j] = kr[...].reshape(2 * ROWS, HD)
        vx[j, :, :HD] = vr[...].reshape(2 * ROWS, HD)
        vx[j, :, HD:] = ones
    for j, (kr, vr) in enumerate(((bo.at[0], bo.at[1]), (bt.at[0, 0], bt.at[0, 1]), (bt.at[1, 0], bt.at[1, 1]))):
        kbx[j] = kr[...].reshape(ROWS, HD)
        vbx[j, :, :HD] = vr[...].reshape(ROWS, HD)
        vbx[j, :, HD:] = ones[:ROWS]
    tx[:, :HD] = text[1]
    tx[:, HD:] = ones[:ROWS]
    mains = [(kx.at[j], vx.at[j], oks[j]) for j in range(3)]
    sides = [(kbx.at[j], vbx.at[j], oks[j]) for j in range(3)]
    texts = [(text.at[0], tx, None)]
    blocks = [(w, role, mains + (sides if role == 0 else []) + (texts if w == 0 else [])) for w in (1, 2, 0) for role in (0, 1)]
    lane = lax.broadcasted_iota(jnp.int32, (ROWS, HD), 1)
    unit = (
        lax.broadcasted_iota(jnp.int32, (16, HD), 0) == lax.broadcasted_iota(jnp.int32, (16, HD), 1)
    ).astype(jnp.float32).astype(jnp.bfloat16)

    def score(block):
        w, role, groups = block
        return [dot_nt(qs[w, role], kr[...]) for kr, _, _ in groups]

    def finish(block, scores):
        w, role, groups = block
        top = None
        for s, (_, _, ok) in zip(scores, groups):
            t = jnp.max(s, axis=1, keepdims=True)
            if ok is not None:
                t = jnp.where(ok, t, NEG)
            top = t if top is None else jnp.maximum(top, t)
        top = top * scale
        acc = None
        for s, (_, vr, ok) in zip(scores, groups):
            t = top if ok is None else jnp.where(ok, top, -NEG)
            p = jnp.exp2(s * scale - t).astype(jnp.bfloat16)
            a = jnp.dot(p, vr[...], preferred_element_type=jnp.float32)
            acc = a if acc is None else acc + a
        summed, total = acc[:, :HD], acc[:, HD:]
        hb = bnd if role == 0 else 1 - bnd
        if w == 0:
            oo[hb] = summed
            os[hb] = jnp.where(lane < 64, top, total)
            return
        out = ol if w == 1 else orr
        out[pl.ds(hb * ROWS, ROWS), :] = summed.astype(jnp.bfloat16)
        parts = jnp.zeros((ROWS, HD), jnp.float32)
        for i, part in enumerate(split3(jnp.broadcast_to(top, (ROWS, HD))) + split3(total)):
            parts = jnp.where(lane == i, part, parts)
        stats = dot_nt(unit, parts.astype(jnp.bfloat16))
        base = 2 * ROWS + 16 * hb
        out[pl.ds(base, 16), :] = jnp.concatenate([stats[:8, :HD], stats[:8, HD:]], 0).astype(jnp.bfloat16)

    held = score(blocks[0])
    for i, block in enumerate(blocks):
        ahead = score(blocks[i + 1]) if i + 1 < len(blocks) else None
        finish(block, held)
        held = ahead


def attend(flags, q, q_left, q_right, k, v, kv_minus, kv_plus, side_own, side_t, text, first, last):
    heads = last - first
    whole = lambda h: (0, 0, 0, first + h)
    part4 = pl.BlockSpec((TILE_T, 2, 64, HD), whole)
    part5 = pl.BlockSpec((2, TILE_T, 2, 64, HD), lambda h: (0, 0, 0, 0, h))
    scale = HD ** (-0.5) * LOG2E
    pairs = heads * ROWS * ROWS * 47
    sent = jax.ShapeDtypeStruct((heads, 2 * ROWS + STAT_ROWS, HD), jnp.bfloat16)
    kept = jax.ShapeDtypeStruct((heads, 2, ROWS, HD), jnp.float32)
    sent_spec = pl.BlockSpec((None, 2 * ROWS + STAT_ROWS, HD), lambda h: (h, 0, 0))
    kept_spec = pl.BlockSpec((None, 2, ROWS, HD), lambda h: (h, 0, 0, 0))
    return pl.pallas_call(
        functools.partial(attend_kernel, scale),
        grid=(heads,),
        in_specs=[
            pl.BlockSpec(memory_space=pltpu.SMEM),
            part4,
            part4,
            part4,
            part4,
            part4,
            part5,
            part5,
            pl.BlockSpec((2, TILE_T, 64, HD), whole),
            pl.BlockSpec((2, 2, TILE_T, 64, HD), lambda h: (0, 0, 0, 0, h)),
            pl.BlockSpec((2, ROWS, HD), lambda h: (0, 0, first + h)),
        ],
        out_specs=[kept_spec, kept_spec, sent_spec, sent_spec],
        out_shape=[kept, kept, sent, sent],
        scratch_shapes=[
            pltpu.VMEM((3, 2, ROWS, HD), jnp.bfloat16),
            pltpu.VMEM((3, 2 * ROWS, HD), jnp.bfloat16),
            pltpu.VMEM((3, 2 * ROWS, 2 * HD), jnp.bfloat16),
            pltpu.VMEM((3, ROWS, HD), jnp.bfloat16),
            pltpu.VMEM((3, ROWS, 2 * HD), jnp.bfloat16),
            pltpu.VMEM((ROWS, 2 * HD), jnp.bfloat16),
        ],
        compiler_params=pltpu.CompilerParams(vmem_limit_bytes=40 << 20),
        cost_estimate=pl.CostEstimate(flops=8 * HD * pairs, bytes_accessed=heads * 3000000, transcendentals=pairs),
        name=f"attend_{first}",
    )(flags, q, q_left, q_right, k, v, kv_minus, kv_plus, side_own, side_t, text)


def combine_kernel(flags, oo, os, ol, orr, *rest):
    out = rest[-1]
    eye = (
        lax.broadcasted_iota(jnp.int32, (HD, HD), 0) == lax.broadcasted_iota(jnp.int32, (HD, HD), 1)
    ).astype(jnp.float32).astype(jnp.bfloat16)
    for hb in range(2):
        tops, totals, sums = [os[hb][:, 0:1]], [os[hb][:, 64:65]], [oo[hb]]
        for ok, ref in ((flags[3] > 0, ol), (flags[4] > 0, orr)):
            base = 2 * ROWS + 16 * hb
            stats = ref[base : base + 16, :]
            cols = dot_nt(eye, stats)
            cols = jnp.concatenate([cols[:, :8], cols[:, 8:16]], 0)
            tops.append(jnp.where(ok, cols[:, 0:1] + cols[:, 1:2] + cols[:, 2:3], NEG))
            totals.append(cols[:, 3:4] + cols[:, 4:5] + cols[:, 5:6])
            sums.append(ref[hb * ROWS : (hb + 1) * ROWS, :].astype(jnp.float32))
        top = jnp.maximum(jnp.maximum(tops[0], tops[1]), tops[2])
        gains = [jnp.exp2(t - top) for t in tops]
        total = sum(g * t for g, t in zip(gains, totals))
        gains = [g / total for g in gains]
        value = sum(jnp.broadcast_to(g, (ROWS, HD)) * s for g, s in zip(gains, sums))
        out[:, hb] = value.astype(jnp.bfloat16).reshape(TILE_T, 64, HD)


def combine(flags, oo, os, o_left, o_right, before, first, last, shape):
    heads = last - first
    sent_spec = pl.BlockSpec((None, 2 * ROWS + STAT_ROWS, HD), lambda h: (h, 0, 0))
    kept_spec = pl.BlockSpec((None, 2, ROWS, HD), lambda h: (h, 0, 0, 0))
    extra = [] if before is None else [before]
    return pl.pallas_call(
        combine_kernel,
        grid=(heads,),
        in_specs=[pl.BlockSpec(memory_space=pltpu.SMEM), kept_spec, kept_spec, sent_spec, sent_spec]
        + [pl.BlockSpec(memory_space=pl.ANY)] * len(extra),
        out_specs=pl.BlockSpec((TILE_T, 2, 64, HD), lambda h: (0, 0, 0, first + h)),
        out_shape=jax.ShapeDtypeStruct(shape, jnp.bfloat16),
        input_output_aliases={5: 0} if extra else {},
        compiler_params=pltpu.CompilerParams(vmem_limit_bytes=20 << 20),
        cost_estimate=pl.CostEstimate(flops=heads * 1000000, bytes_accessed=heads * 1000000, transcendentals=0),
        name=f"combine_{first}",
    )(flags, oo, os, o_left, o_right, *extra)


def steps(axis):
    size = lax.axis_size(axis)
    up = [(i, i + 1) for i in range(size - 1)]
    return up, [(j, i) for i, j in up]


def per_device(queries, keys, values, text_keys, text_values):
    chans = queries.shape[3]
    shape = (TILE_T, 2, TILE_H * TILE_W, chans)
    q, k, v = (a.reshape(shape) for a in (queries, keys, values))
    ta, ha, wa = (lax.axis_index(a) for a in ("ta", "ha", "wa"))
    last_t, last_w = lax.axis_size("ta") - 1, lax.axis_size("wa") - 1
    side = 1 - ha
    flags = jnp.stack([side, ta > 0, ta < last_t, wa > 0, wa < last_w]).astype(jnp.int32)
    t_up, t_down = steps("ta")
    w_up, w_down = steps("wa")
    swap = [(0, 1), (1, 0)]

    rows = text_keys.shape[0]
    pad = jnp.zeros((TEXT_PAD, chans), jnp.bfloat16)
    text = lax.all_gather(jnp.concatenate([text_keys, text_values, pad], 0), ("ta", "ha", "wa"))
    text = jnp.stack([text[:, :rows].reshape(-1, chans), text[:, rows : 2 * rows].reshape(-1, chans)])

    halo = []
    for first, last in CHUNKS:
        both = jnp.stack([k[..., first * HD : last * HD], v[..., first * HD : last * HD]])
        halo.append((lax.ppermute(both, "ta", t_up), lax.ppermute(both, "ta", t_down)))
    q_left = lax.ppermute(q, "wa", w_up)
    q_right = lax.ppermute(q, "wa", w_down)
    pick = lambda a, axis: lax.dynamic_index_in_dim(a, side, axis, keepdims=False)
    side_own = lax.ppermute(jnp.stack([pick(k, 1), pick(v, 1)]), "ha", swap)

    out = None
    for (first, last), (minus, plus) in zip(CHUNKS, halo):
        side_t = lax.ppermute(jnp.stack([pick(minus, 2), pick(plus, 2)]), "ha", swap)
        oo, os, ol, orr = attend(flags, q, q_left, q_right, k, v, minus, plus, side_own, side_t, text, first, last)
        from_right = lax.ppermute(ol, "wa", w_down)
        from_left = lax.ppermute(orr, "wa", w_up)
        out = combine(flags, oo, os, from_left, from_right, out, first, last, shape)
    return out.reshape(queries.shape)


def solution(mesh):
    placed = (
        P("ta", "ha", "wa", None),
        P("ta", "ha", "wa", None),
        P("ta", "ha", "wa", None),
        P(("ta", "ha", "wa"), None),
        P(("ta", "ha", "wa"), None),
    )
    return jax.shard_map(
        per_device, mesh=mesh, in_specs=placed, out_specs=P("ta", "ha", "wa", None), check_vma=False
    )
```

```python
import functools

import jax
import jax.numpy as jnp
from jax import lax
from jax.experimental import pallas as pl
from jax.experimental.pallas import tpu as pltpu
from jax.sharding import PartitionSpec as P

HEADS = 6
TILE_T = 4
TILE_H = 8
TILE_W = 8
HD = 128
ROWS = 256
STEP = 256
MAIN = 6 * ROWS
SIDE = 3 * ROWS
STAT_ROWS = 32
LOG2E = 1.4426950408889634
NEG = -1e30
CHUNKS = ((0, 3), (3, 6))
ALL_AXES = ("ta", "ha", "wa")


def dot_nt(a, b):
    return lax.dot_general(a, b, (((1,), (1,)), ((), ())), preferred_element_type=jnp.float32)


def unit(rows):
    row = lax.broadcasted_iota(jnp.int32, (rows, HD), 0)
    col = lax.broadcasted_iota(jnp.int32, (rows, HD), 1)
    return (row == col).astype(jnp.float32).astype(jnp.bfloat16)


def fill_keys(ks, vs, base, k, v, minus, plus, side_own, side_minus, side_plus):
    pieces = [(k[...], v[...]), (minus[0], minus[1]), (plus[0], plus[1])]
    pieces += [(s[0], s[1]) for s in (side_own, side_minus, side_plus)]
    at = base
    for kk, vv in pieces:
        rows = kk.size // HD
        ks[at : at + rows] = kk.reshape(rows, HD)
        vs[at : at + rows, :HD] = vv.reshape(rows, HD)
        at += rows
    vs[:, HD:] = jnp.ones((vs.shape[0], HD), jnp.bfloat16)


def soft_step(scale, flags, qs, ks, vs, held, text, emit):
    oks = [None, flags[1] > 0, flags[2] > 0]
    count = qs.shape[0] // STEP

    def cuts(i):
        sizes = [(text, None)] if text else []
        sizes += [(2 * ROWS, ok) for ok in oks]
        if i < count // 2:
            sizes += [(ROWS, ok) for ok in oks]
        out, at = [], 0
        for n, ok in sizes:
            out.append((at, at + n, ok))
            at += n
        return out, at

    def score(i):
        parts, n = cuts(i)
        rows = slice(i * STEP, (i + 1) * STEP)
        s = dot_nt(qs[rows], ks[:n])
        held[rows, :n] = s
        top = None
        for a, b, ok in parts:
            t = s[:, a : a + HD]
            for c in range(a + HD, b, HD):
                t = jnp.maximum(t, s[:, c : c + HD])
            if ok is not None:
                t = jnp.where(ok, t, NEG)
            top = t if top is None else jnp.maximum(top, t)
        top = jnp.max(top, axis=1, keepdims=True) * scale
        return top.astype(jnp.bfloat16).astype(jnp.float32)

    def finish(i, top):
        parts, n = cuts(i)
        rows = slice(i * STEP, (i + 1) * STEP)
        ps = []
        for a, b, ok in parts:
            t = top if ok is None else jnp.where(ok, top, -NEG)
            ps.append(jnp.exp2(held[rows, a:b] * scale - t).astype(jnp.bfloat16))
        acc = jnp.dot(jnp.concatenate(ps, 1), vs[:n], preferred_element_type=jnp.float32)
        emit(i, top, acc[:, HD:], acc[:, :HD])

    top = score(0)
    for i in range(count):
        ahead = score(i + 1) if i + 1 < count else None
        finish(i, top)
        top = ahead


def guest_kernel(scale, flags, ql, qr, k, v, minus, plus, so, sm, sp, ol, orr, ks, vs, qs, held, stats):
    head, heads = pl.program_id(0), pl.num_programs(0)
    bnd = flags[0]
    tiles = [(ref, out, hb) for hb in (bnd, 1 - bnd) for ref, out in ((ql, 0), (qr, 1))]
    for i, (ref, _, hb) in enumerate(tiles):
        qs[i * ROWS : (i + 1) * ROWS] = ref[:, hb].reshape(ROWS, HD)
    fill_keys(ks, vs, 0, k, v, minus, plus, so, sm, sp)

    @pl.when(head == 0)
    def _():
        stats[...] = jnp.zeros(stats.shape, stats.dtype)

    lane = lax.broadcasted_iota(jnp.int32, (STEP, HD), 1)
    outs = (ol, orr)

    def emit(i, top, total, summed):
        _, out, hb = tiles[i * STEP // ROWS]
        part = i * STEP % ROWS
        high = total.astype(jnp.bfloat16).astype(jnp.float32)
        outs[out][pl.ds((head * 2 + hb) * ROWS + part, STEP), :] = summed.astype(jnp.bfloat16)
        at = lane - (head * 2 + hb) * 8
        kept = jnp.where(at == 0, top, stats[out, part : part + STEP])
        kept = jnp.where(at == 1, high, kept)
        stats[out, part : part + STEP] = jnp.where(at == 2, total - high, kept)

    soft_step(scale, flags, qs, ks, vs, held, 0, emit)

    @pl.when(head == heads - 1)
    def _():
        count = ol.shape[0] // (2 * ROWS + STAT_ROWS) * 2
        for i, out in enumerate(outs):
            rows = dot_nt(unit(HD), stats[i].astype(jnp.bfloat16))
            for j in range(count):
                pair = [rows[8 * j : 8 * j + 8, :HD], rows[8 * j : 8 * j + 8, HD:]]
                at = count * ROWS + 16 * j
                out[at : at + 16, :] = jnp.concatenate(pair, 0).astype(jnp.bfloat16)


def own_kernel(scale, flags, q, k, v, minus, plus, so, sm, sp, tk, tv, ol, orr, *rest):
    out, ks, vs, qs, held, cols = rest[-6:]
    bnd, head = flags[0], pl.program_id(0)
    for i in range(2):
        qs[i * ROWS : (i + 1) * ROWS] = q[:, bnd if i == 0 else 1 - bnd].reshape(ROWS, HD)
    ks[:ROWS] = tk[...]
    vs[:ROWS, :HD] = tv[...]
    fill_keys(ks, vs, ROWS, k, v, minus, plus, so, sm, sp)

    @pl.when(head == 0)
    def _():
        count = ol.shape[0] // (2 * ROWS + STAT_ROWS) * 2
        for i, ref in enumerate((ol, orr)):
            for j in range(count):
                at = count * ROWS + 16 * j
                pair = dot_nt(unit(HD), ref[at : at + 16, :])
                cols[i, j] = jnp.concatenate([pair[:, :8], pair[:, 8:16]], 0)

    def emit(j, top, total, summed):
        hb = bnd if j * STEP < ROWS else 1 - bnd
        part = j * STEP % ROWS
        tops, totals, sums = [top], [total[:, :1]], [summed]
        for i, (ok, ref) in enumerate(((flags[3] > 0, ol), (flags[4] > 0, orr))):
            col = cols[i, head * 2 + hb, part : part + STEP]
            tops.append(jnp.where(ok, col[:, 0:1], NEG))
            totals.append(col[:, 1:2] + col[:, 2:3])
            sums.append(ref[pl.ds((head * 2 + hb) * ROWS + part, STEP), :].astype(jnp.float32))
        best = jnp.maximum(jnp.maximum(tops[0], tops[1]), tops[2])
        gains = [jnp.exp2(t - best) for t in tops]
        whole = gains[0] * totals[0] + gains[1] * totals[1] + gains[2] * totals[2]
        value = sum(jnp.broadcast_to(g / whole, (STEP, HD)) * s for g, s in zip(gains, sums))
        first = part // 64
        out[first : first + STEP // 64, hb] = value.astype(jnp.bfloat16).reshape(STEP // 64, 64, HD)

    soft_step(scale, flags, qs, ks, vs, held, ROWS, emit)


def call(kernel, name, flags, first, last, wholes, pairs5, sides5, more, more_specs, out_shape, out_specs, keys, rows, scratch, share, aliases):
    heads = last - first
    part4 = pl.BlockSpec((TILE_T, 2, 64, HD), lambda h, f: (0, 0, 0, first + h))
    part5 = pl.BlockSpec((2, TILE_T, 2, 64, HD), lambda h, f: (0, 0, 0, 0, h))
    side5 = pl.BlockSpec((2, TILE_T, None, 64, HD), lambda h, f: (0, 0, 1 - f[0], 0, h))
    pairs = heads * ROWS * ROWS * share
    return pl.pallas_call(
        functools.partial(kernel, HD ** (-0.5) * LOG2E),
        grid_spec=pltpu.PrefetchScalarGridSpec(
            num_scalar_prefetch=1,
            grid=(heads,),
            in_specs=[part4] * len(wholes) + [part5] * len(pairs5) + [side5] * len(sides5) + more_specs,
            out_specs=out_specs,
            scratch_shapes=[
                pltpu.VMEM((keys, HD), jnp.bfloat16),
                pltpu.VMEM((keys, 2 * HD), jnp.bfloat16),
                pltpu.VMEM((rows, HD), jnp.bfloat16),
                pltpu.VMEM((rows, keys), jnp.float32),
            ]
            + scratch,
        ),
        out_shape=out_shape,
        input_output_aliases=aliases,
        compiler_params=pltpu.CompilerParams(vmem_limit_bytes=56 << 20),
        cost_estimate=pl.CostEstimate(flops=8 * HD * pairs, bytes_accessed=heads * 2000000, transcendentals=pairs),
        name=f"{name}_{first}",
    )(flags, *wholes, *pairs5, *sides5, *more)


def sent_rows(first, last):
    return (last - first) * (2 * ROWS + STAT_ROWS)


def sent_spec(first, last):
    return pl.BlockSpec((sent_rows(first, last), HD), lambda h, f: (0, 0))


def guests(flags, q_left, q_right, k, v, halo, sides, first, last):
    sent = jax.ShapeDtypeStruct((sent_rows(first, last), HD), jnp.bfloat16)
    spec = sent_spec(first, last)
    scratch = [pltpu.VMEM((2, ROWS, HD), jnp.float32)]
    return call(
        guest_kernel, "guests", flags, first, last, (q_left, q_right, k, v), halo, sides, (), [],
        [sent, sent], [spec, spec], MAIN + SIDE, 4 * ROWS, scratch, 30, {},
    )


def owns(flags, q, k, v, halo, sides, text, o_left, o_right, before, first, last):
    heads = last - first
    specs = [
        pl.BlockSpec((ROWS, HD), lambda h, f: (0, first + h)),
        pl.BlockSpec((ROWS, HD), lambda h, f: (0, HEADS + first + h)),
        sent_spec(first, last),
        sent_spec(first, last),
    ]
    more = (text, text, o_left, o_right)
    aliases = {}
    if before is not None:
        more += (before,)
        specs.append(pl.BlockSpec(memory_space=pl.ANY))
        aliases = {13: 0}
    return call(
        own_kernel, "owns", flags, first, last, (q, k, v), halo, sides, more, specs,
        jax.ShapeDtypeStruct(q.shape, jnp.bfloat16),
        pl.BlockSpec((TILE_T, 2, 64, HD), lambda h, f: (0, 0, 0, first + h)),
        ROWS + MAIN + SIDE, 2 * ROWS, [pltpu.VMEM((2, 2 * heads, ROWS, 8), jnp.float32)], 17, aliases,
    )


def steps(axis):
    size = lax.axis_size(axis)
    up = [(i, i + 1) for i in range(size - 1)]
    return up, [(j, i) for i, j in up]


def per_device(queries, keys, values, text_keys, text_values):
    chans = queries.shape[3]
    shape = (TILE_T, 2, TILE_H * TILE_W, chans)
    q, k, v = (a.reshape(shape) for a in (queries, keys, values))
    ta, ha, wa = (lax.axis_index(a) for a in ALL_AXES)
    last_t, last_w = lax.axis_size("ta") - 1, lax.axis_size("wa") - 1
    flags = jnp.stack([1 - ha, ta > 0, ta < last_t, wa > 0, wa < last_w]).astype(jnp.int32)
    t_up, t_down = steps("ta")
    w_up, w_down = steps("wa")
    swap = lambda a: lax.ppermute(a, "ha", [(0, 1), (1, 0)])

    q_left = lax.ppermute(q, "wa", w_up)
    q_right = lax.ppermute(q, "wa", w_down)
    pairs = [jnp.stack([k[..., a * HD : b * HD], v[..., a * HD : b * HD]]) for a, b in CHUNKS]
    own_sides = [swap(pairs[0])]
    for i in range(1, len(pairs)):
        own_sides[-1], pairs[i] = lax.optimization_barrier((own_sides[-1], pairs[i]))
        own_sides.append(swap(pairs[i]))
    halos = [(lax.ppermute(p, "ta", t_up), lax.ppermute(p, "ta", t_down)) for p in pairs]

    count = lax.axis_size(ALL_AXES)
    text = jnp.concatenate([text_keys, text_values], 1)
    text = jnp.broadcast_to(text[None], (count,) + text.shape)
    text = lax.all_to_all(text, ALL_AXES, 0, 0, tiled=False).reshape(-1, 2 * chans)

    halos[0], text = lax.optimization_barrier((halos[0], text))
    returned, sides = [], []
    for i, ((first, last), pair) in enumerate(zip(CHUNKS, pairs)):
        halo = halos[i]
        if i > 0:
            halo, _ = halos[i], _ = lax.optimization_barrier((halo, (ol, orr)))
        sides.append((own_sides[i], swap(halo[0]), swap(halo[1])))
        ol, orr = guests(flags, q_left, q_right, k, v, halo, sides[-1], first, last)
        returned.append((lax.ppermute(orr, "wa", w_up), lax.ppermute(ol, "wa", w_down)))
    out = None
    for (first, last), halo, side, (o_left, o_right) in zip(CHUNKS, halos, sides, returned):
        out = owns(flags, q, k, v, halo, side, text, o_left, o_right, out, first, last)
    return out.reshape(queries.shape)


def solution(mesh):
    placed = (
        P("ta", "ha", "wa", None),
        P("ta", "ha", "wa", None),
        P("ta", "ha", "wa", None),
        P(("ta", "ha", "wa"), None),
        P(("ta", "ha", "wa"), None),
    )
    return jax.shard_map(
        per_device, mesh=mesh, in_specs=placed, out_specs=P("ta", "ha", "wa", None), check_vma=False
    )
```

```python
import functools

import jax
import jax.numpy as jnp
from jax import lax
from jax.experimental import pallas as pl
from jax.experimental.pallas import tpu as pltpu
from jax.sharding import PartitionSpec as P

HEADS = 6
TILE_T = 4
TILE_H = 8
TILE_W = 8
HD = 128
ROWS = 256
STEP = 256
MAIN = 6 * ROWS
SIDE = 3 * ROWS
STAT_ROWS = 32
LOG2E = 1.4426950408889634
NEG = -1e30
CHUNKS = ((0, 3), (3, 6))
ALL_AXES = ("ta", "ha", "wa")


def dot_nt(a, b):
    return lax.dot_general(a, b, (((1,), (1,)), ((), ())), preferred_element_type=jnp.float32)


def unit(rows):
    row = lax.broadcasted_iota(jnp.int32, (rows, HD), 0)
    col = lax.broadcasted_iota(jnp.int32, (rows, HD), 1)
    return (row == col).astype(jnp.float32).astype(jnp.bfloat16)


def fill_keys(ks, vs, base, k, v, minus, plus, side_own, side_minus, side_plus):
    pieces = [(k[...], v[...]), (minus[0], minus[1]), (plus[0], plus[1])]
    pieces += [(s[0], s[1]) for s in (side_own, side_minus, side_plus)]
    at = base
    for kk, vv in pieces:
        rows = kk.size // HD
        ks[at : at + rows] = kk.reshape(rows, HD)
        vs[at : at + rows, :HD] = vv.reshape(rows, HD)
        at += rows
    vs[:, HD:] = jnp.ones((vs.shape[0], HD), jnp.bfloat16)


def soft_step(scale, flags, qs, ks, vs, held, text, emit, exact):
    oks = [None, flags[1] > 0, flags[2] > 0]
    count = qs.shape[0] // STEP

    def cuts(i):
        sizes = [(text, None)] if text else []
        sizes += [(2 * ROWS, ok) for ok in oks]
        if i < count // 2:
            sizes += [(ROWS, ok) for ok in oks]
        out, at = [], 0
        for n, ok in sizes:
            out.append((at, at + n, ok))
            at += n
        return out, at

    def score(i):
        parts, n = cuts(i)
        rows = slice(i * STEP, (i + 1) * STEP)
        s = dot_nt(qs[rows], ks[:n])
        held[rows, :n] = s
        top = None
        for a, b, ok in parts:
            t = s[:, a : a + HD]
            for c in range(a + HD, b, HD):
                t = jnp.maximum(t, s[:, c : c + HD])
            if ok is not None:
                t = jnp.where(ok, t, NEG)
            top = t if top is None else jnp.maximum(top, t)
        top = jnp.max(top, axis=1, keepdims=True) * scale
        return top if exact else top.astype(jnp.bfloat16).astype(jnp.float32)

    def finish(i, top):
        parts, n = cuts(i)
        rows = slice(i * STEP, (i + 1) * STEP)
        ps = []
        for a, b, ok in parts:
            t = top if ok is None else jnp.where(ok, top, -NEG)
            ps.append(jnp.exp2(held[rows, a:b] * scale - t).astype(jnp.bfloat16))
        acc = jnp.dot(jnp.concatenate(ps, 1), vs[:n], preferred_element_type=jnp.float32)
        emit(i, top, acc[:, HD:], acc[:, :HD])

    top = score(0)
    for i in range(count):
        ahead = score(i + 1) if i + 1 < count else None
        finish(i, top)
        top = ahead


def guest_kernel(scale, flags, ql, qr, k, v, minus, plus, so, sm, sp, ol, orr, ks, vs, qs, held, stats):
    head, heads = pl.program_id(0), pl.num_programs(0)
    bnd = flags[0]
    tiles = [(ref, out, hb) for hb in (bnd, 1 - bnd) for ref, out in ((ql, 0), (qr, 1))]
    for i, (ref, _, hb) in enumerate(tiles):
        qs[i * ROWS : (i + 1) * ROWS] = ref[:, hb].reshape(ROWS, HD)
    fill_keys(ks, vs, 0, k, v, minus, plus, so, sm, sp)

    @pl.when(head == 0)
    def _():
        stats[...] = jnp.zeros(stats.shape, stats.dtype)

    lane = lax.broadcasted_iota(jnp.int32, (STEP, HD), 1)
    outs = (ol, orr)

    def emit(i, top, total, summed):
        _, out, hb = tiles[i * STEP // ROWS]
        part = i * STEP % ROWS
        high = total.astype(jnp.bfloat16).astype(jnp.float32)
        outs[out][pl.ds((head * 2 + hb) * ROWS + part, STEP), :] = summed.astype(jnp.bfloat16)
        at = lane - (head * 2 + hb) * 8
        kept = jnp.where(at == 0, top, stats[out, part : part + STEP])
        kept = jnp.where(at == 1, high, kept)
        stats[out, part : part + STEP] = jnp.where(at == 2, total - high, kept)

    soft_step(scale, flags, qs, ks, vs, held, 0, emit, False)

    @pl.when(head == heads - 1)
    def _():
        count = ol.shape[0] // (2 * ROWS + STAT_ROWS) * 2
        for i, out in enumerate(outs):
            rows = dot_nt(unit(HD), stats[i].astype(jnp.bfloat16))
            for j in range(count):
                pair = [rows[8 * j : 8 * j + 8, :HD], rows[8 * j : 8 * j + 8, HD:]]
                at = count * ROWS + 16 * j
                out[at : at + 16, :] = jnp.concatenate(pair, 0).astype(jnp.bfloat16)


def own_kernel(scale, flags, q, k, v, minus, plus, so, sm, sp, tk, tv, ol, orr, *rest):
    out, ks, vs, qs, held, cols = rest[-6:]
    bnd, head = flags[0], pl.program_id(0)
    for i in range(2):
        qs[i * ROWS : (i + 1) * ROWS] = q[:, bnd if i == 0 else 1 - bnd].reshape(ROWS, HD)
    ks[:ROWS] = tk[...]
    vs[:ROWS, :HD] = tv[...]
    fill_keys(ks, vs, ROWS, k, v, minus, plus, so, sm, sp)

    @pl.when(head == 0)
    def _():
        count = ol.shape[0] // (2 * ROWS + STAT_ROWS) * 2
        for i, ref in enumerate((ol, orr)):
            for j in range(count):
                at = count * ROWS + 16 * j
                pair = dot_nt(unit(HD), ref[at : at + 16, :])
                cols[i, j] = jnp.concatenate([pair[:, :8], pair[:, 8:16]], 0)

    def emit(j, top, total, summed):
        hb = bnd if j * STEP < ROWS else 1 - bnd
        part = j * STEP % ROWS
        tops, totals, sums = [top], [total[:, :1]], [summed]
        for i, (ok, ref) in enumerate(((flags[3] > 0, ol), (flags[4] > 0, orr))):
            col = cols[i, head * 2 + hb, part : part + STEP]
            tops.append(jnp.where(ok, col[:, 0:1], NEG))
            totals.append(col[:, 1:2] + col[:, 2:3])
            sums.append(ref[pl.ds((head * 2 + hb) * ROWS + part, STEP), :].astype(jnp.float32))
        best = jnp.maximum(jnp.maximum(tops[0], tops[1]), tops[2])
        gains = [jnp.exp2(t - best) for t in tops]
        whole = gains[0] * totals[0] + gains[1] * totals[1] + gains[2] * totals[2]
        value = sum(jnp.broadcast_to(g / whole, (STEP, HD)) * s for g, s in zip(gains, sums))
        first = part // 64
        out[first : first + STEP // 64, hb] = value.astype(jnp.bfloat16).reshape(STEP // 64, 64, HD)

    soft_step(scale, flags, qs, ks, vs, held, ROWS, emit, True)


def call(kernel, name, flags, first, last, wholes, pairs5, sides5, more, more_specs, out_shape, out_specs, keys, rows, scratch, share, aliases):
    heads = last - first
    part4 = pl.BlockSpec((TILE_T, 2, 64, HD), lambda h, f: (0, 0, 0, first + h))
    part5 = pl.BlockSpec((2, TILE_T, 2, 64, HD), lambda h, f: (0, 0, 0, 0, h))
    side5 = pl.BlockSpec((2, TILE_T, None, 64, HD), lambda h, f: (0, 0, 1 - f[0], 0, h))
    pairs = heads * ROWS * ROWS * share
    return pl.pallas_call(
        functools.partial(kernel, HD ** (-0.5) * LOG2E),
        grid_spec=pltpu.PrefetchScalarGridSpec(
            num_scalar_prefetch=1,
            grid=(heads,),
            in_specs=[part4] * len(wholes) + [part5] * len(pairs5) + [side5] * len(sides5) + more_specs,
            out_specs=out_specs,
            scratch_shapes=[
                pltpu.VMEM((keys, HD), jnp.bfloat16),
                pltpu.VMEM((keys, 2 * HD), jnp.bfloat16),
                pltpu.VMEM((rows, HD), jnp.bfloat16),
                pltpu.VMEM((rows, keys), jnp.float32),
            ]
            + scratch,
        ),
        out_shape=out_shape,
        input_output_aliases=aliases,
        compiler_params=pltpu.CompilerParams(vmem_limit_bytes=56 << 20),
        cost_estimate=pl.CostEstimate(flops=8 * HD * pairs, bytes_accessed=heads * 2000000, transcendentals=pairs),
        name=f"{name}_{first}",
    )(flags, *wholes, *pairs5, *sides5, *more)


def sent_rows(first, last):
    return (last - first) * (2 * ROWS + STAT_ROWS)


def sent_spec(first, last):
    return pl.BlockSpec((sent_rows(first, last), HD), lambda h, f: (0, 0))


def guests(flags, q_left, q_right, k, v, halo, sides, first, last):
    sent = jax.ShapeDtypeStruct((sent_rows(first, last), HD), jnp.bfloat16)
    spec = sent_spec(first, last)
    scratch = [pltpu.VMEM((2, ROWS, HD), jnp.float32)]
    return call(
        guest_kernel, "guests", flags, first, last, (q_left, q_right, k, v), halo, sides, (), [],
        [sent, sent], [spec, spec], MAIN + SIDE, 4 * ROWS, scratch, 30, {},
    )


def owns(flags, q, k, v, halo, sides, text, o_left, o_right, before, first, last):
    heads = last - first
    specs = [
        pl.BlockSpec((ROWS, HD), lambda h, f: (0, first + h)),
        pl.BlockSpec((ROWS, HD), lambda h, f: (0, HEADS + first + h)),
        sent_spec(first, last),
        sent_spec(first, last),
    ]
    more = (text, text, o_left, o_right)
    aliases = {}
    if before is not None:
        more += (before,)
        specs.append(pl.BlockSpec(memory_space=pl.ANY))
        aliases = {13: 0}
    return call(
        own_kernel, "owns", flags, first, last, (q, k, v), halo, sides, more, specs,
        jax.ShapeDtypeStruct(q.shape, jnp.bfloat16),
        pl.BlockSpec((TILE_T, 2, 64, HD), lambda h, f: (0, 0, 0, first + h)),
        ROWS + MAIN + SIDE, 2 * ROWS, [pltpu.VMEM((2, 2 * heads, ROWS, 8), jnp.float32)], 17, aliases,
    )


def steps(axis):
    size = lax.axis_size(axis)
    up = [(i, i + 1) for i in range(size - 1)]
    return up, [(j, i) for i, j in up]


def per_device(queries, keys, values, text_keys, text_values):
    chans = queries.shape[3]
    shape = (TILE_T, 2, TILE_H * TILE_W, chans)
    q, k, v = (a.reshape(shape) for a in (queries, keys, values))
    ta, ha, wa = (lax.axis_index(a) for a in ALL_AXES)
    last_t, last_w = lax.axis_size("ta") - 1, lax.axis_size("wa") - 1
    flags = jnp.stack([1 - ha, ta > 0, ta < last_t, wa > 0, wa < last_w]).astype(jnp.int32)
    t_up, t_down = steps("ta")
    w_up, w_down = steps("wa")
    swap = lambda a: lax.ppermute(a, "ha", [(0, 1), (1, 0)])

    q_left = lax.ppermute(q, "wa", w_up)
    q_right = lax.ppermute(q, "wa", w_down)
    pairs = [jnp.stack([k[..., a * HD : b * HD], v[..., a * HD : b * HD]]) for a, b in CHUNKS]
    own_sides = [swap(pairs[0])]
    for i in range(1, len(pairs)):
        own_sides[-1], pairs[i] = lax.optimization_barrier((own_sides[-1], pairs[i]))
        own_sides.append(swap(pairs[i]))
    halos = [(lax.ppermute(p, "ta", t_up), lax.ppermute(p, "ta", t_down)) for p in pairs]

    text_pair = jnp.concatenate([text_keys, text_values], 1)
    text_pair = jnp.broadcast_to(text_pair[None], (lax.axis_size(ALL_AXES),) + text_pair.shape)
    returned, sides = [], []
    for i, ((first, last), pair) in enumerate(zip(CHUNKS, pairs)):
        halo = halos[i]
        if i > 0:
            halo, _ = halos[i], _ = lax.optimization_barrier((halo, (ol, orr)))
        sides.append((own_sides[i], swap(halo[0]), swap(halo[1])))
        ol, orr = guests(flags, q_left, q_right, k, v, halo, sides[-1], first, last)
        if i == 0:
            ol, orr, text_pair = lax.optimization_barrier((ol, orr, text_pair))
        returned.append((lax.ppermute(orr, "wa", w_up), lax.ppermute(ol, "wa", w_down)))
    text = lax.all_to_all(text_pair, ALL_AXES, 0, 0, tiled=False).reshape(-1, 2 * chans)
    out = None
    for (first, last), halo, side, (o_left, o_right) in zip(CHUNKS, halos, sides, returned):
        out = owns(flags, q, k, v, halo, side, text, o_left, o_right, out, first, last)
    return out.reshape(queries.shape)


def solution(mesh):
    placed = (
        P("ta", "ha", "wa", None),
        P("ta", "ha", "wa", None),
        P("ta", "ha", "wa", None),
        P(("ta", "ha", "wa"), None),
        P(("ta", "ha", "wa"), None),
    )
    return jax.shard_map(
        per_device, mesh=mesh, in_specs=placed, out_specs=P("ta", "ha", "wa", None), check_vma=False
    )
```

```python
import functools

import jax
import jax.numpy as jnp
from jax import lax
from jax.experimental import pallas as pl
from jax.experimental.pallas import tpu as pltpu
from jax.sharding import PartitionSpec as P

HEADS = 6
TILE_T = 4
TILE_H = 8
TILE_W = 8
HD = 128
ROWS = 256
STEP = 256
MAIN = 6 * ROWS
SIDE = 3 * ROWS
STAT_ROWS = 32
LOG2E = 1.4426950408889634
NEG = -1e30
CHUNKS = ((0, 3), (3, 6))
ALL_AXES = ("ta", "ha", "wa")


def dot_nt(a, b):
    return lax.dot_general(a, b, (((1,), (1,)), ((), ())), preferred_element_type=jnp.float32)


def unit(rows):
    row = lax.broadcasted_iota(jnp.int32, (rows, HD), 0)
    col = lax.broadcasted_iota(jnp.int32, (rows, HD), 1)
    return (row == col).astype(jnp.float32).astype(jnp.bfloat16)


def fill_keys(ks, vs, base, k, v, minus, plus, side_own, side_minus, side_plus):
    pieces = [(k[...], v[...]), (minus[0], minus[1]), (plus[0], plus[1])]
    pieces += [(s[0], s[1]) for s in (side_own, side_minus, side_plus)]
    at = base
    for kk, vv in pieces:
        rows = kk.size // HD
        ks[at : at + rows] = kk.reshape(rows, HD)
        vs[at : at + rows, :HD] = vv.reshape(rows, HD)
        at += rows

    @pl.when(pl.program_id(0) == 0)
    def _():
        vs[:, HD:] = jnp.ones((vs.shape[0], HD), jnp.bfloat16)


def soft_step(scale, flags, qs, ks, vs, held, text, emit, exact):
    oks = [None, flags[1] > 0, flags[2] > 0]
    count = qs.shape[0] // STEP

    def cuts(i):
        sizes = [(text, None)] if text else []
        sizes += [(2 * ROWS, ok) for ok in oks]
        if i < count // 2:
            sizes += [(ROWS, ok) for ok in oks]
        out, at = [], 0
        for n, ok in sizes:
            out.append((at, at + n, ok))
            at += n
        return out, at

    def score(i):
        parts, n = cuts(i)
        rows = slice(i * STEP, (i + 1) * STEP)
        s = dot_nt(qs[rows], ks[:n])
        held[rows, :n] = s
        top = None
        for a, b, ok in parts:
            t = s[:, a : a + HD]
            for c in range(a + HD, b, HD):
                t = jnp.maximum(t, s[:, c : c + HD])
            if ok is not None:
                t = jnp.where(ok, t, NEG)
            top = t if top is None else jnp.maximum(top, t)
        top = jnp.max(top, axis=1, keepdims=True) * scale
        return top if exact else top.astype(jnp.bfloat16).astype(jnp.float32)

    def finish(i, top):
        parts, n = cuts(i)
        rows = slice(i * STEP, (i + 1) * STEP)
        ps = []
        for a, b, ok in parts:
            t = top if ok is None else jnp.where(ok, top, -NEG)
            ps.append(jnp.exp2(held[rows, a:b] * scale - t).astype(jnp.bfloat16))
        acc = jnp.dot(jnp.concatenate(ps, 1), vs[:n], preferred_element_type=jnp.float32)
        emit(i, top, acc[:, HD:], acc[:, :HD])

    top = score(0)
    for i in range(count):
        ahead = score(i + 1) if i + 1 < count else None
        finish(i, top)
        top = ahead


def guest_kernel(scale, flags, ql, qr, k, v, minus, plus, so, sm, sp, ol, orr, ks, vs, qs, held, stats):
    head, heads = pl.program_id(0), pl.num_programs(0)
    bnd = flags[0]
    tiles = [(ref, out, hb) for hb in (bnd, 1 - bnd) for ref, out in ((ql, 0), (qr, 1))]
    for i, (ref, _, hb) in enumerate(tiles):
        qs[i * ROWS : (i + 1) * ROWS] = ref[:, hb].reshape(ROWS, HD)
    fill_keys(ks, vs, 0, k, v, minus, plus, so, sm, sp)

    @pl.when(head == 0)
    def _():
        stats[...] = jnp.zeros(stats.shape, stats.dtype)

    lane = lax.broadcasted_iota(jnp.int32, (STEP, HD), 1)
    outs = (ol, orr)

    def emit(i, top, total, summed):
        _, out, hb = tiles[i * STEP // ROWS]
        part = i * STEP % ROWS
        high = total.astype(jnp.bfloat16).astype(jnp.float32)
        outs[out][pl.ds((head * 2 + hb) * ROWS + part, STEP), :] = summed.astype(jnp.bfloat16)
        at = lane - (head * 2 + hb) * 8
        kept = jnp.where(at == 0, top, stats[out, part : part + STEP])
        kept = jnp.where(at == 1, high, kept)
        stats[out, part : part + STEP] = jnp.where(at == 2, total - high, kept)

    soft_step(scale, flags, qs, ks, vs, held, 0, emit, False)

    @pl.when(head == heads - 1)
    def _():
        count = ol.shape[0] // (2 * ROWS + STAT_ROWS) * 2
        for i, out in enumerate(outs):
            rows = dot_nt(unit(HD), stats[i].astype(jnp.bfloat16))
            for j in range(count):
                pair = [rows[8 * j : 8 * j + 8, :HD], rows[8 * j : 8 * j + 8, HD:]]
                at = count * ROWS + 16 * j
                out[at : at + 16, :] = jnp.concatenate(pair, 0).astype(jnp.bfloat16)


def own_kernel(scale, flags, q, k, v, minus, plus, so, sm, sp, tk, tv, ol, orr, *rest):
    out, ks, vs, qs, held, cols = rest[-6:]
    bnd, head = flags[0], pl.program_id(0)
    for i in range(2):
        qs[i * ROWS : (i + 1) * ROWS] = q[:, bnd if i == 0 else 1 - bnd].reshape(ROWS, HD)
    ks[:ROWS] = tk[...]
    vs[:ROWS, :HD] = tv[...]
    fill_keys(ks, vs, ROWS, k, v, minus, plus, so, sm, sp)

    @pl.when(head == 0)
    def _():
        count = ol.shape[0] // (2 * ROWS + STAT_ROWS) * 2
        for i, ref in enumerate((ol, orr)):
            for j in range(count):
                at = count * ROWS + 16 * j
                pair = dot_nt(unit(HD), ref[at : at + 16, :])
                cols[i, j] = jnp.concatenate([pair[:, :8], pair[:, 8:16]], 0)

    def emit(j, top, total, summed):
        hb = bnd if j * STEP < ROWS else 1 - bnd
        part = j * STEP % ROWS
        tops, totals, sums = [top], [total[:, :1]], [summed]
        for i, (ok, ref) in enumerate(((flags[3] > 0, ol), (flags[4] > 0, orr))):
            col = cols[i, head * 2 + hb, part : part + STEP]
            tops.append(jnp.where(ok, col[:, 0:1], NEG))
            totals.append(col[:, 1:2] + col[:, 2:3])
            sums.append(ref[pl.ds((head * 2 + hb) * ROWS + part, STEP), :].astype(jnp.float32))
        best = jnp.maximum(jnp.maximum(tops[0], tops[1]), tops[2])
        gains = [jnp.exp2(t - best) for t in tops]
        whole = gains[0] * totals[0] + gains[1] * totals[1] + gains[2] * totals[2]
        value = sum(jnp.broadcast_to(g / whole, (STEP, HD)) * s for g, s in zip(gains, sums))
        first = part // 64
        out[first : first + STEP // 64, hb] = value.astype(jnp.bfloat16).reshape(STEP // 64, 64, HD)

    soft_step(scale, flags, qs, ks, vs, held, ROWS, emit, True)


def call(kernel, name, flags, first, last, wholes, pairs5, sides5, more, more_specs, out_shape, out_specs, keys, rows, scratch, share, aliases):
    heads = last - first
    part4 = pl.BlockSpec((TILE_T, 2, 64, HD), lambda h, f: (0, 0, 0, first + h))
    part5 = pl.BlockSpec((2, TILE_T, 2, 64, HD), lambda h, f: (0, 0, 0, 0, h))
    side5 = pl.BlockSpec((2, TILE_T, None, 64, HD), lambda h, f: (0, 0, 1 - f[0], 0, h))
    pairs = heads * ROWS * ROWS * share
    return pl.pallas_call(
        functools.partial(kernel, HD ** (-0.5) * LOG2E),
        grid_spec=pltpu.PrefetchScalarGridSpec(
            num_scalar_prefetch=1,
            grid=(heads,),
            in_specs=[part4] * len(wholes) + [part5] * len(pairs5) + [side5] * len(sides5) + more_specs,
            out_specs=out_specs,
            scratch_shapes=[
                pltpu.VMEM((keys, HD), jnp.bfloat16),
                pltpu.VMEM((keys, 2 * HD), jnp.bfloat16),
                pltpu.VMEM((rows, HD), jnp.bfloat16),
                pltpu.VMEM((rows, keys), jnp.float32),
            ]
            + scratch,
        ),
        out_shape=out_shape,
        input_output_aliases=aliases,
        compiler_params=pltpu.CompilerParams(vmem_limit_bytes=56 << 20),
        cost_estimate=pl.CostEstimate(flops=8 * HD * pairs, bytes_accessed=heads * 2000000, transcendentals=pairs),
        name=f"{name}_{first}",
    )(flags, *wholes, *pairs5, *sides5, *more)


def sent_rows(first, last):
    return (last - first) * (2 * ROWS + STAT_ROWS)


def sent_spec(first, last):
    return pl.BlockSpec((sent_rows(first, last), HD), lambda h, f: (0, 0))


def guests(flags, q_left, q_right, k, v, halo, sides, first, last):
    sent = jax.ShapeDtypeStruct((sent_rows(first, last), HD), jnp.bfloat16)
    spec = sent_spec(first, last)
    scratch = [pltpu.VMEM((2, ROWS, HD), jnp.float32)]
    return call(
        guest_kernel, "guests", flags, first, last, (q_left, q_right, k, v), halo, sides, (), [],
        [sent, sent], [spec, spec], MAIN + SIDE, 4 * ROWS, scratch, 30, {},
    )


def owns(flags, q, k, v, halo, sides, text, o_left, o_right, before, first, last):
    heads = last - first
    specs = [
        pl.BlockSpec((ROWS, HD), lambda h, f: (0, first + h)),
        pl.BlockSpec((ROWS, HD), lambda h, f: (0, HEADS + first + h)),
        sent_spec(first, last),
        sent_spec(first, last),
    ]
    more = (text, text, o_left, o_right)
    aliases = {}
    if before is not None:
        more += (before,)
        specs.append(pl.BlockSpec(memory_space=pl.ANY))
        aliases = {13: 0}
    return call(
        own_kernel, "owns", flags, first, last, (q, k, v), halo, sides, more, specs,
        jax.ShapeDtypeStruct(q.shape, jnp.bfloat16),
        pl.BlockSpec((TILE_T, 2, 64, HD), lambda h, f: (0, 0, 0, first + h)),
        ROWS + MAIN + SIDE, 2 * ROWS, [pltpu.VMEM((2, 2 * heads, ROWS, 8), jnp.float32)], 17, aliases,
    )


def steps(axis):
    size = lax.axis_size(axis)
    up = [(i, i + 1) for i in range(size - 1)]
    return up, [(j, i) for i, j in up]


def per_device(queries, keys, values, text_keys, text_values):
    chans = queries.shape[3]
    shape = (TILE_T, 2, TILE_H * TILE_W, chans)
    q, k, v = (a.reshape(shape) for a in (queries, keys, values))
    ta, ha, wa = (lax.axis_index(a) for a in ALL_AXES)
    last_t, last_w = lax.axis_size("ta") - 1, lax.axis_size("wa") - 1
    flags = jnp.stack([1 - ha, ta > 0, ta < last_t, wa > 0, wa < last_w]).astype(jnp.int32)
    t_up, t_down = steps("ta")
    w_up, w_down = steps("wa")
    swap = lambda a: lax.ppermute(a, "ha", [(0, 1), (1, 0)])

    q_left = lax.ppermute(q, "wa", w_up)
    q_right = lax.ppermute(q, "wa", w_down)
    pairs = [jnp.stack([k[..., a * HD : b * HD], v[..., a * HD : b * HD]]) for a, b in CHUNKS]
    own_sides = [swap(pairs[0])]
    for i in range(1, len(pairs)):
        own_sides[-1], pairs[i] = lax.optimization_barrier((own_sides[-1], pairs[i]))
        own_sides.append(swap(pairs[i]))
    halos = [(lax.ppermute(p, "ta", t_up), lax.ppermute(p, "ta", t_down)) for p in pairs]

    text_pair = jnp.concatenate([text_keys, text_values], 1)
    text_pair = jnp.broadcast_to(text_pair[None], (lax.axis_size(ALL_AXES),) + text_pair.shape)
    returned, sides = [], []
    for i, ((first, last), pair) in enumerate(zip(CHUNKS, pairs)):
        halo = halos[i]
        if i > 0:
            halo, _ = halos[i], _ = lax.optimization_barrier((halo, (ol, orr)))
        sides.append((own_sides[i], swap(halo[0]), swap(halo[1])))
        ol, orr = guests(flags, q_left, q_right, k, v, halo, sides[-1], first, last)
        if i == 0:
            ol, orr, text_pair = lax.optimization_barrier((ol, orr, text_pair))
        returned.append((lax.ppermute(orr, "wa", w_up), lax.ppermute(ol, "wa", w_down)))
    text = lax.all_to_all(text_pair, ALL_AXES, 0, 0, tiled=False).reshape(-1, 2 * chans)
    out = None
    for (first, last), halo, side, (o_left, o_right) in zip(CHUNKS, halos, sides, returned):
        out = owns(flags, q, k, v, halo, side, text, o_left, o_right, out, first, last)
    return out.reshape(queries.shape)


def solution(mesh):
    placed = (
        P("ta", "ha", "wa", None),
        P("ta", "ha", "wa", None),
        P("ta", "ha", "wa", None),
        P(("ta", "ha", "wa"), None),
        P(("ta", "ha", "wa"), None),
    )
    return jax.shard_map(
        per_device, mesh=mesh, in_specs=placed, out_specs=P("ta", "ha", "wa", None), check_vma=False
    )
```
